1024 devices in a mesh: ctx: 128 (over y, z), tp: 8 (over x, core).
Axes of the slice: x: 4, y: 8, z: 16, core: 2. Of those that a mesh axis runs over, the one named last changes fastest.
Arguments:
- query: bfloat16 [32768, 8192], P('ctx', 'tp'), may hold values from -6 to 6
- gated: bfloat16 [32768, 8192], P('ctx', 'tp'), may hold values from -6 to 6
- cotangent: bfloat16 [32768, 8192], P('ctx', 'tp'), may hold values from -6 to 6
- rate: float32 [8192, 8], P('tp'), may hold values from 1e-08 to 0.03
- residue: float32 [8192, 8], P('tp'), may hold values from -2 to 2
- gain: float32 [8192], P('tp'), may hold values from 0.5 to 1.5
Outputs:
- normed: bfloat16 [32768, 8192], P('ctx', 'tp')
- query_grad: bfloat16 [32768, 8192], P('ctx', 'tp')
- gated_grad: bfloat16 [32768, 8192], P('ctx', 'tp')
The draws below stay inside these ranges and needn't reach their ends.
All inputs are finite; a program needn't handle non-finite values.
Results may differ from the reference program's by a relative error of at most 0.0015.
Values sent between devices are 32-bit elements; how exact they have to be, the bound alone decides.
A program may use at most 64 MiB of HBM per device.

```python
import math
import jax
import jax.numpy as jnp
from jax import lax

CH = 8192
ORDER = 8
SEQ = 32768


def block_scale(key, shape, shards, low, top_value):
    factor_of, own = 1.0, jax.random.fold_in(key, 6)
    for position, blocks in shards:
        steps = jnp.exp(jax.random.uniform(jax.random.fold_in(own, position), (blocks,), jnp.float32, low / len(shards), top_value / len(shards)))
        factor_of = factor_of * jnp.repeat(steps, shape[position] // blocks).reshape([-1 if axis == position else 1 for axis in range(len(shape))])
    return factor_of


def scatter_about(stream_key, extent, deviation, limit, pieces=(), dtype=jnp.bfloat16):
    array = deviation * jax.random.normal(stream_key, extent, jnp.float32)
    if pieces:
        array = array * block_scale(stream_key, extent, pieces, -0.22, 0.18)
    return jnp.clip(array, -limit, limit).astype(dtype)


def setup_inputs(seed: int = 0) -> dict:
    arg_keys = jax.random.split(jax.random.key(seed), 7)
    query = scatter_about(arg_keys[0], (SEQ, CH), 1.0, 6.0, ((0, 128), (1, 8)))
    gated = scatter_about(arg_keys[1], (SEQ, CH), 1.0, 6.0, ((0, 128), (1, 8)))
    cotangent = scatter_about(arg_keys[2], (SEQ, CH), 1.0, 6.0, ((0, 128), (1, 8)))
    rate = jnp.clip(jnp.exp(math.log(0.03) - 14.914123 * jax.random.uniform(arg_keys[3], (CH, ORDER), jnp.float32) ** block_scale(arg_keys[3], (CH, ORDER), ((0, 8),), -0.2, 0.2)), 9.99999993922529e-09, 0.03)
    residue = scatter_about(arg_keys[4], (CH, ORDER), ORDER ** -0.5, 2.0, ((0, 8),), jnp.float32)
    gain = jnp.clip(1.0 + 0.1 * jax.random.normal(arg_keys[5], (CH,), jnp.float32), 0.5, 1.5)
    return dict(query=query, gated=gated, cotangent=cotangent, rate=rate, residue=residue, gain=gain)


def reference(query, gated, cotangent, rate, residue, gain):
    hp = lax.Precision.HIGHEST
    blk = 16
    weight = residue * jnp.sqrt(2.0 * rate + 1.0 / SEQ)
    pos = jnp.arange(blk).astype(jnp.float32)
    lam_pow = jnp.exp(-rate[None] * pos[:, None, None])
    hvals = lax.optimization_barrier(jnp.sum(lam_pow * weight[None], axis=-1))
    diff = jnp.arange(blk)[:, None] - jnp.arange(blk)[None, :]
    index = jnp.clip(diff, 0, blk - 1).astype(jnp.int32)
    toep = jnp.where((diff >= 0)[:, :, None], hvals[index], 0.0)
    step_decay = jnp.exp(-rate * blk)
    into = jnp.exp(-rate[None] * (pos[:, None, None] + 1.0)) * weight[None]
    back_tab = jnp.exp(-rate[None] * (blk - pos)[:, None, None]) * weight[None]
    ends_tab = lam_pow[::-1]
    blocks = gated.astype(jnp.float32).reshape(SEQ // blk, blk, CH)

    def fstep(state, ublk):
        zblk = jnp.einsum('tsc,sc->tc', toep, ublk, precision=hp)
        zblk = zblk + jnp.einsum('cm,tcm->tc', state, into, precision=hp)
        state = step_decay * state + jnp.einsum('sc,scm->cm', ublk, ends_tab, precision=hp)
        return (state, zblk)
    _, conv = lax.scan(fstep, jnp.zeros((CH, ORDER), jnp.float32), blocks)
    conv = conv.reshape(SEQ, CH)
    qf = query.astype(jnp.float32)
    mixed = qf * conv
    inv_rms = 1.0 / jnp.sqrt(lax.optimization_barrier(jnp.mean(mixed * mixed, axis=1, keepdims=True)) + 1e-06)
    normed = (mixed * inv_rms * gain[None]).astype(jnp.bfloat16)
    scaled = gain[None] * cotangent.astype(jnp.float32)
    proj = lax.optimization_barrier(jnp.mean(scaled * mixed, axis=1, keepdims=True))
    mixed_grad = inv_rms * scaled - mixed * inv_rms ** 3 * proj
    query_grad = (mixed_grad * conv).astype(jnp.bfloat16)
    conv_grad = (mixed_grad * qf).reshape(SEQ // blk, blk, CH)

    def bstep(state, dblk):
        gblk = jnp.einsum('tsc,tc->sc', toep, dblk, precision=hp)
        gblk = gblk + jnp.einsum('cm,scm->sc', state, back_tab, precision=hp)
        state = step_decay * state + jnp.einsum('tc,tcm->cm', dblk, lam_pow, precision=hp)
        return (state, gblk)
    _, gated_grad = lax.scan(bstep, jnp.zeros((CH, ORDER), jnp.float32), conv_grad, reverse=True)
    return (normed, query_grad, gated_grad.reshape(SEQ, CH).astype(jnp.bfloat16))
```

```python
import functools

import jax
import jax.numpy as jnp
from jax import lax
from jax.experimental import pallas as pl
from jax.experimental.pallas import tpu as pltpu
from jax.sharding import PartitionSpec as P

MESH = pl.DeviceIdType.MESH
NJ = 4
MODES = 8
SUB = 8
LANES = 128
F32 = jnp.float32


def kernel(
    ny, nk, ntp,
    query, gated, cotangent, rate, residue, gain,
    normed, query_grad, gated_grad,
    qb, gb, cb, rate_v, residue_v, gain_v,
    u, y, qf, sf, cg, nm, qg,
    rt, lam_t, w_t, cf_t, cb_t, ex_t,
    states, incoming, z1_buf, z2_buf, y_buf, g_out, t_out, in_out,
    sq, cs, msg, tp_buf, inv_t, proj_t,
    in_sem, out_sem, send_sem, recv_sem, tp_send, tp_recv,
):
    tokens, width = qb.shape
    groups = width // LANES
    part = groups // NJ
    steps = tokens // SUB
    seq_total = tokens * NJ * nk * ny
    total_width = width * ntp
    place = lax.axis_index("ctx")
    column = lax.axis_index("tp")
    yy = place // (NJ * nk)
    kk = lax.rem(place // NJ, nk)
    jj = lax.rem(place, NJ)

    def at(y_, k_, j_):
        return (y_ * nk + k_) * NJ + j_

    near = [at(yy, kk, lax.rem(jj + i, NJ)) for i in range(1, NJ)]
    across = [at(yy, lax.rem(kk + i, nk), jj) for i in range(1, nk)]
    rows = [at(lax.rem(yy + i, ny), kk, jj) for i in range(1, ny)]
    mates = [lax.rem(column + i, ntp) for i in range(1, ntp)]

    barrier = pltpu.get_barrier_semaphore()
    for other in near + across + rows:
        pl.semaphore_signal(barrier, inc=1, device_id=(other, column), device_id_type=MESH)
    for mate in mates:
        pl.semaphore_signal(barrier, inc=1, device_id=(place, mate), device_id_type=MESH)

    loads = [
        pltpu.make_async_copy(src, dst, in_sem.at[n])
        for n, (src, dst) in enumerate(
            [(rate, rate_v), (residue, residue_v), (gated, gb), (query, qb), (cotangent, cb), (gain, gain_v)]
        )
    ]
    for load in loads:
        load.start()

    seg = lax.broadcasted_iota(jnp.int32, (SUB, LANES), 0)
    segf = seg.astype(F32)
    lane = lax.broadcasted_iota(jnp.int32, (SUB, LANES), 1)

    def cols(c):
        return pl.ds(pl.multiple_of(c * LANES, LANES), LANES)

    def wide(row):
        return jnp.broadcast_to(row, (SUB, LANES))

    def token_rows(j):
        return pl.ds(j, SUB, stride=steps)

    def spread(src, dst, scale=None):
        @pl.loop(0, groups)
        def _(c):
            for t in range(0, tokens, 32):
                tile = src[t : t + 32, cols(c)].astype(F32)
                dst[c, t : t + 32, :] = tile if scale is None else tile * scale[pl.ds(c, 1), :]

    def gather_segments(c, state, reverse):
        for m in range(MODES):
            r = wide(rate_v[pl.ds(m, 1), cols(c)])
            x = state[m]
            for hop in (1, 2, 4):
                decay = jnp.exp(-r * float(steps * hop))
                if reverse:
                    x = x + jnp.where(seg < SUB - hop, decay, 0.0) * pltpu.roll(x, SUB - hop, 0)
                else:
                    x = x + jnp.where(seg >= hop, decay, 0.0) * pltpu.roll(x, hop, 0)
            if reverse:
                states[1, c, pl.ds(m, 1), :] = x[0:1]
                ex_t[c, m] = jnp.where(seg < SUB - 1, pltpu.roll(x, SUB - 1, 0), 0.0)
            else:
                states[0, c, pl.ds(m, 1), :] = x[SUB - 1 : SUB]
                ex_t[c, m] = jnp.where(seg >= 1, pltpu.roll(x, 1, 0), 0.0)

    def add_up(terms):
        while len(terms) > 1:
            terms = [a + b for a, b in zip(terms[::2], terms[1::2])] + ([terms[-1]] if len(terms) % 2 else [])
        return terms[0]

    loads[0].wait()
    loads[1].wait()

    @pl.loop(0, groups)
    def _(c):
        rates = rate_v[:, cols(c)]
        rt[c] = rates
        residue_v[:, cols(c)] = residue_v[:, cols(c)] * jnp.sqrt(2.0 * rates + 1.0 / seq_total)
        for m in range(MODES):
            lam_t[c, m] = jnp.exp(-wide(rate_v[pl.ds(m, 1), cols(c)]))

    loads[2].wait()
    spread(gb, u)

    @pl.loop(0, groups)
    def _(c):
        lam = [lam_t[c, m] for m in range(MODES)]

        def block(jb, state):
            for inner in range(4):
                value = u[c, token_rows(jb * 4 + inner), :]
                state = [lam[m] * state[m] + value for m in range(MODES)]
            return state

        state = lax.fori_loop(0, steps // 4, block, [jnp.zeros((SUB, LANES), F32)] * MODES)
        gather_segments(c, state, False)

    pl.semaphore_wait(barrier, len(near) + len(across) + len(rows) + len(mates))

    sends = []

    def copy(src, dst, way, number, device):
        out = pltpu.make_async_remote_copy(
            src_ref=src,
            dst_ref=dst,
            send_sem=send_sem.at[way, number],
            recv_sem=recv_sem.at[way, number],
            device_id=device,
            device_id_type=MESH,
        )
        sends.append(out)
        return out

    def exchange(way):
        mirror = lambda p, n: (n - 1 - p) if way else p
        slot = lambda p, i, n: lax.rem(p + n - i, n)
        j_me, k_me, y_me = mirror(jj, NJ), mirror(kk, nk), mirror(yy, ny)
        j_src = [mirror(slot(jj, i, NJ), NJ) for i in range(NJ)]
        k_src = [mirror(slot(kk, i, nk), nk) for i in range(nk)]
        y_src = [mirror(slot(yy, i, ny), ny) for i in range(ny)]
        quarter = pl.ds(jj * part, part)

        def decay(blocks):
            count = (blocks * tokens).astype(F32) if hasattr(blocks, "astype") else float(blocks * tokens)
            return jnp.exp(-rt[quarter] * count)

        def before(source, here, blocks_apart):
            gap = jnp.maximum(here - source - 1, 0)
            return jnp.where(source < here, decay(gap * blocks_apart), 0.0)

        first = [
            copy(
                states.at[way, pl.ds(lax.rem(jj + i, NJ) * part, part)],
                z1_buf.at[way, i - 1], way, i - 1, (near[i - 1], column),
            )
            for i in range(1, NJ)
        ]
        for one in first:
            one.start()
        yield
        weights = [decay(NJ - 1 - j_src[i]) for i in range(NJ)]
        own = states[way, quarter]
        for one in first:
            one.wait_recv()
        members = [own] + [z1_buf[way, i] for i in range(NJ - 1)]
        total = add_up([a * b for a, b in zip(weights, members)])
        g_out[way] = total
        base = NJ - 1
        second = [
            copy(g_out.at[way], z2_buf.at[way, i - 1], way, base + i - 1, (across[i - 1], column))
            for i in range(1, nk)
        ]
        for one in second:
            one.start()
        yield
        within = []
        for i in range(NJ):
            target = mirror(lax.rem(jj + i, NJ), NJ)
            within.append((target, add_up([before(j_src[s], target, 1) * members[s] for s in range(NJ)])))
        weights = [decay(NJ * (nk - 1 - k_src[i])) for i in range(nk)]
        ahead = [before(k_src[i], k_me, NJ) for i in range(nk)]
        for one in second:
            one.wait_recv()
        totals = [total] + [z2_buf[way, i] for i in range(nk - 1)]
        row = add_up([a * b for a, b in zip(weights, totals)])
        t_out[way] = row
        base = base + nk - 1
        third = [
            copy(t_out.at[way], y_buf.at[way, i - 1], way, base + i - 1, (rows[i - 1], column))
            for i in range(1, ny)
        ]
        for one in third:
            one.start()
        yield
        in_row = add_up([a * b for a, b in zip(ahead, totals)])
        weights = [before(y_src[i], y_me, NJ * nk) for i in range(ny)]
        to_group = decay(NJ * k_me)
        reach = [decay(target) for target, _ in within]
        for one in third:
            one.wait_recv()
        rows_in = [row] + [y_buf[way, i] for i in range(ny - 1)]
        enters = in_row + to_group * add_up([a * b for a, b in zip(weights, rows_in)])
        base = base + ny - 1
        fourth = []
        for i in range(NJ):
            result = within[i][1] + reach[i] * enters
            if i == 0:
                incoming[way, quarter] = result
            else:
                in_out[way, i - 1] = result
                one = copy(
                    in_out.at[way, i - 1], incoming.at[way, quarter],
                    way, base + i - 1, (near[i - 1], column),
                )
                one.start()
                fourth.append(one)
        yield
        for one in fourth:
            one.wait_recv()
        yield

    forward = exchange(0)
    next(forward)

    @pl.loop(0, groups)
    def _(c):
        for m in range(MODES):
            w = wide(residue_v[pl.ds(m, 1), cols(c)])
            r = wide(rate_v[pl.ds(m, 1), cols(c)])
            w_t[c, m] = w
            cf_t[c, m] = w * jnp.exp(-r * (segf * float(steps) + 1.0))
            cb_t[c, m] = w * jnp.exp(-r * (float(tokens - steps + 1) - segf * float(steps)))

    next(forward)

    @pl.loop(0, groups)
    def _(c):
        lam = [lam_t[c, m] for m in range(MODES)]
        w = [w_t[c, m] for m in range(MODES)]

        def block(jb, state):
            for inner in range(4):
                j = jb * 4 + inner
                value = u[c, token_rows(j), :]
                state = [lam[m] * state[m] + value for m in range(MODES)]
                y[c, token_rows(j), :] = add_up([w[m] * state[m] for m in range(MODES)])
            return state

        lax.fori_loop(0, steps // 4, block, [ex_t[c, m] for m in range(MODES)])

    next(forward)
    for load in loads[3:]:
        load.wait()
    spread(qb, qf)
    spread(cb, sf, gain_v)
    sq[...] = jnp.zeros_like(sq)
    cs[...] = jnp.zeros_like(cs)
    next(forward)
    next(forward)

    @pl.loop(0, groups)
    def _(c):
        lam = [lam_t[c, m] for m in range(MODES)]
        start = [cf_t[c, m] * wide(incoming[0, c, pl.ds(m, 1), :]) for m in range(MODES)]

        def block(jb, state):
            for inner in range(4):
                j = jb * 4 + inner
                at_j = token_rows(j)
                conv = y[c, at_j, :] + add_up(state)
                state = [lam[m] * state[m] for m in range(MODES)]
                y[c, at_j, :] = conv
                mixed = qf[c, at_j, :] * conv
                sq[j] = sq[j] + mixed * mixed
                cs[j] = cs[j] + sf[c, at_j, :] * mixed
            return state

        lax.fori_loop(0, steps // 4, block, start)

    packed = jnp.zeros((SUB, LANES), F32)

    def pack(jb, packed):
        for inner in range(4):
            j = jb * 4 + inner
            packed = jnp.where(lane == j, jnp.sum(sq[j], axis=1, keepdims=True), packed)
            packed = jnp.where(lane == j + steps, jnp.sum(cs[j], axis=1, keepdims=True), packed)
        return packed

    packed = lax.fori_loop(0, steps // 4, pack, packed)
    msg[...] = packed
    posts = [
        pltpu.make_async_remote_copy(
            src_ref=msg,
            dst_ref=tp_buf.at[i - 1],
            send_sem=tp_send.at[i - 1],
            recv_sem=tp_recv.at[i - 1],
            device_id=(place, mates[i - 1]),
            device_id_type=MESH,
        )
        for i in range(1, ntp)
    ]
    for post in posts:
        post.start()
    for post in posts:
        post.wait_recv()
    sends.extend(posts)
    sums = add_up([packed] + [tp_buf[i] for i in range(ntp - 1)]) * (1.0 / total_width)
    inv = 1.0 / jnp.sqrt(sums + 1e-06)
    proj = pltpu.roll(sums, LANES - steps, 1) * (inv * inv * inv)
    for j in range(steps):
        inv_t[j] = jnp.broadcast_to(inv[:, j : j + 1], (SUB, LANES))
        proj_t[j] = jnp.broadcast_to(proj[:, j : j + 1], (SUB, LANES))

    @pl.loop(0, groups)
    def _(c):
        lam = [lam_t[c, m] for m in range(MODES)]

        def block(jb, state):
            for inner in range(4):
                j = steps - 1 - (jb * 4 + inner)
                at_j = token_rows(j)
                q = qf[c, at_j, :]
                mixed = q * y[c, at_j, :]
                value = (inv_t[j] * sf[c, at_j, :] - mixed * proj_t[j]) * q
                cg[c, at_j, :] = value
                state = [lam[m] * state[m] + value for m in range(MODES)]
            return state

        state = lax.fori_loop(0, steps // 4, block, [jnp.zeros((SUB, LANES), F32)] * MODES)
        gather_segments(c, state, True)

    backward = exchange(1)
    next(backward)

    @pl.loop(0, groups)
    def _(c):
        lam = [lam_t[c, m] for m in range(MODES)]
        w = [w_t[c, m] for m in range(MODES)]

        def block(jb, state):
            for inner in range(4):
                j = steps - 1 - (jb * 4 + inner)
                at_j = token_rows(j)
                value = cg[c, at_j, :]
                state = [lam[m] * state[m] + value for m in range(MODES)]
                u[c, at_j, :] = add_up([w[m] * state[m] for m in range(MODES)])
            return state

        lax.fori_loop(0, steps // 4, block, [ex_t[c, m] for m in range(MODES)])

    next(backward)

    @pl.loop(0, groups)
    def _(c):
        scale = wide(gain_v[pl.ds(c, 1), :])

        def block(jb, carry):
            for inner in range(4):
                j = jb * 4 + inner
                at_j = token_rows(j)
                conv = y[c, at_j, :]
                mixed = qf[c, at_j, :] * conv
                inv_j = inv_t[j]
                nm[c, at_j, :] = mixed * inv_j * scale
                qg[c, at_j, :] = (inv_j * sf[c, at_j, :] - mixed * proj_t[j]) * conv
            return carry

        lax.fori_loop(0, steps // 4, block, 0)

    next(backward)

    def round_out(src, dst):
        @pl.loop(0, groups)
        def _(c):
            for t in range(0, tokens, 32):
                dst[t : t + 32, cols(c)] = src[c, t : t + 32, :].astype(dst.dtype)

    round_out(nm, gb)
    store_normed = pltpu.make_async_copy(gb, normed, out_sem.at[0])
    store_normed.start()
    round_out(qg, cb)
    store_query = pltpu.make_async_copy(cb, query_grad, out_sem.at[1])
    store_query.start()
    next(backward)
    next(backward)

    @pl.loop(0, groups)
    def _(c):
        lam = [lam_t[c, m] for m in range(MODES)]
        start = [cb_t[c, m] * wide(incoming[1, c, pl.ds(m, 1), :]) for m in range(MODES)]

        def block(jb, state):
            for inner in range(4):
                j = steps - 1 - (jb * 4 + inner)
                at_j = token_rows(j)
                u[c, at_j, :] = u[c, at_j, :] + add_up(state)
                state = [lam[m] * state[m] for m in range(MODES)]
            return state

        lax.fori_loop(0, steps // 4, block, start)

    round_out(u, qb)
    store_gated = pltpu.make_async_copy(qb, gated_grad, out_sem.at[2])
    store_gated.start()
    for one in sends:
        one.wait_send()
    store_normed.wait()
    store_query.wait()
    store_gated.wait()


def shape_of(ctx):
    return (8, 4) if ctx == 128 else (2, ctx // (2 * NJ))


def solution(mesh):
    ntp, ctx = mesh.shape["tp"], mesh.shape["ctx"]
    ny, nk = shape_of(ctx)

    def per_device(query, gated, cotangent, rate, residue, gain):
        tokens, width = query.shape
        groups = width // LANES
        part = groups // NJ
        steps = tokens // SUB
        vmem = lambda *shape: pltpu.VMEM(shape, F32)
        half = pltpu.VMEM((tokens, width), jnp.bfloat16)
        copies = 2 * (NJ - 1) + (nk - 1) + (ny - 1)
        anywhere = pl.BlockSpec(memory_space=pl.ANY)
        return pl.pallas_call(
            functools.partial(kernel, ny, nk, ntp),
            out_shape=[jax.ShapeDtypeStruct((tokens, width), jnp.bfloat16)] * 3,
            in_specs=[anywhere] * 6,
            out_specs=[anywhere] * 3,
            scratch_shapes=[half] * 3
            + [vmem(MODES, width), vmem(MODES, width), vmem(groups, LANES)]
            + [vmem(groups, tokens, LANES)] * 7
            + [vmem(groups, MODES, LANES)]
            + [vmem(groups, MODES, SUB, LANES)] * 5
            + [
                vmem(2, groups, MODES, LANES),
                vmem(2, groups, MODES, LANES),
                vmem(2, NJ - 1, part, MODES, LANES),
                vmem(2, max(nk - 1, 1), part, MODES, LANES),
                vmem(2, max(ny - 1, 1), part, MODES, LANES),
                vmem(2, part, MODES, LANES),
                vmem(2, part, MODES, LANES),
                vmem(2, NJ - 1, part, MODES, LANES),
            ]
            + [vmem(steps, SUB, LANES)] * 2
            + [vmem(SUB, LANES), vmem(max(ntp - 1, 1), SUB, LANES)]
            + [vmem(steps, SUB, LANES)] * 2
            + [
                pltpu.SemaphoreType.DMA((6,)),
                pltpu.SemaphoreType.DMA((3,)),
                pltpu.SemaphoreType.DMA((2, copies)),
                pltpu.SemaphoreType.DMA((2, copies)),
                pltpu.SemaphoreType.DMA((max(ntp - 1, 1),)),
                pltpu.SemaphoreType.DMA((max(ntp - 1, 1),)),
            ],
            compiler_params=pltpu.CompilerParams(collective_id=0, has_side_effects=True),
            name="hyena",
        )(query, gated, cotangent, rate.T, residue.T, gain.reshape(groups, LANES))

    return jax.shard_map(
        per_device,
        mesh=mesh,
        in_specs=(P("ctx", "tp"), P("ctx", "tp"), P("ctx", "tp"), P("tp", None), P("tp", None), P("tp")),
        out_specs=(P("ctx", "tp"),) * 3,
        check_vma=False,
    )
```

```python
import functools

import jax
import jax.numpy as jnp
from jax import lax
from jax.experimental import pallas as pl
from jax.experimental.pallas import tpu as pltpu
from jax.sharding import PartitionSpec as P

MESH = pl.DeviceIdType.MESH
MODES = 8
SUB = 8
LANES = 128
PAD = 4
PARTS = 4
STEP = 8
F32 = jnp.float32


def add_up(terms):
    while len(terms) > 1:
        terms = [a + b for a, b in zip(terms[::2], terms[1::2])] + ([terms[-1]] if len(terms) % 2 else [])
    return terms[0]


def kernel(
    ny, nz, ntp,
    query, gated, cotangent, rate, residue, gain,
    normed, query_grad, u, behind, lam_t, cb_t,
    qb, gb, cb, rate_v, residue_v, gain_v,
    y, qf, sf, cg, nm, qg,
    rt, w_t, cf_t, ex_t,
    states, incoming, z_buf, y_buf, t_out, in_out, p_buf,
    sq, cs, msg, tp_buf, inv_t, proj_t,
    in_sem, send_sem, recv_sem, tp_send, tp_recv,
):
    tokens, width = qb.shape
    groups = width // LANES
    steps = tokens // SUB
    seq_total = tokens * nz * ny
    total_width = width * ntp
    place = lax.axis_index("ctx")
    column = lax.axis_index("tp")
    yy = place // nz
    zz = lax.rem(place, nz)

    def at(y_, z_):
        return y_ * nz + z_

    z_targets = [lax.rem(zz + i, nz) for i in range(1, nz)]
    y_targets = [lax.rem(yy + i, ny) for i in range(1, ny)]
    mates = [lax.rem(column + i, ntp) for i in range(1, ntp)]

    barrier = pltpu.get_barrier_semaphore()
    for other in [at(yy, z) for z in z_targets] + [at(y_, zz) for y_ in y_targets]:
        pl.semaphore_signal(barrier, inc=1, device_id=(other, column), device_id_type=MESH)
    for mate in mates:
        pl.semaphore_signal(barrier, inc=1, device_id=(place, mate), device_id_type=MESH)

    loads = [
        pltpu.make_async_copy(src, dst, in_sem.at[n])
        for n, (src, dst) in enumerate(
            [(rate, rate_v), (residue, residue_v), (gated, gb), (query, qb), (cotangent, cb), (gain, gain_v)]
        )
    ]
    for load in loads:
        load.start()

    seg = lax.broadcasted_iota(jnp.int32, (SUB, LANES), 0)
    segf = seg.astype(F32)
    lane = lax.broadcasted_iota(jnp.int32, (SUB, LANES), 1)

    def cols(c):
        return pl.ds(pl.multiple_of(c * LANES, LANES), LANES)

    def wide(row):
        return jnp.broadcast_to(row, (SUB, LANES))

    def token_rows(j):
        return pl.ds(j, SUB, stride=steps + PAD)

    def spread(src, dst, scale=None):
        @pl.loop(0, groups)
        def _(c):
            for n in range(SUB):
                tile = src[n * steps : (n + 1) * steps, cols(c)].astype(F32)
                dst[c, pl.ds(n * (steps + PAD), steps), :] = tile if scale is None else tile * scale[pl.ds(c, 1), :]

    def gather_segments(c, state, reverse):
        for m in range(MODES):
            r = wide(rate_v[pl.ds(m, 1), cols(c)])
            x = state[m]
            for hop in (1, 2, 4):
                decay = jnp.exp(-r * float(steps * hop))
                if reverse:
                    x = x + jnp.where(seg < SUB - hop, decay, 0.0) * pltpu.roll(x, SUB - hop, 0)
                else:
                    x = x + jnp.where(seg >= hop, decay, 0.0) * pltpu.roll(x, hop, 0)
            if reverse:
                states[1, c, pl.ds(m, 1), :] = x[0:1]
                ex_t[c, m] = jnp.where(seg < SUB - 1, pltpu.roll(x, SUB - 1, 0), 0.0)
            else:
                states[0, c, pl.ds(m, 1), :] = x[SUB - 1 : SUB]
                ex_t[c, m] = jnp.where(seg >= 1, pltpu.roll(x, 1, 0), 0.0)

    def decays(c):
        lam = [lam_t[c, m] for m in range(MODES)]
        lam4 = [a * a for a in lam]
        return lam, [a * a for a in lam4]

    def accumulate(lam, lam4, state, values):
        for n in range(0, len(values), 4):
            fresh = [
                (lam[m] * values[n] + values[n + 1]) * (lam[m] * lam[m]) + (lam[m] * values[n + 2] + values[n + 3])
                for m in range(MODES)
            ]
            state = [lam4[m] * state[m] + fresh[m] for m in range(MODES)]
        return state

    loads[0].wait()
    loads[1].wait()

    @pl.loop(0, groups)
    def _(c):
        rates = rate_v[:, cols(c)]
        rt[c] = rates
        residue_v[:, cols(c)] = residue_v[:, cols(c)] * jnp.sqrt(2.0 * rates + 1.0 / seq_total)
        for m in range(MODES):
            lam_t[c, m] = jnp.exp(-wide(rate_v[pl.ds(m, 1), cols(c)]))

    loads[2].wait()
    spread(gb, u)

    @pl.loop(0, groups)
    def _(c):
        lam, lam4 = decays(c)

        def block(jb, state):
            values = [u[c, token_rows(jb * STEP + n), :] for n in range(STEP)]
            return accumulate(lam, lam4, state, values)

        state = lax.fori_loop(0, steps // STEP, block, [jnp.zeros((SUB, LANES), F32)] * MODES)
        gather_segments(c, state, False)

    pl.semaphore_wait(barrier, len(z_targets) + len(y_targets) + len(mates))

    sends = []

    def copy(src, dst, way, number, device):
        out = pltpu.make_async_remote_copy(
            src_ref=src,
            dst_ref=dst,
            send_sem=send_sem.at[way, number],
            recv_sem=recv_sem.at[way, number],
            device_id=device,
            device_id_type=MESH,
        )
        sends.append(out)
        return out

    def exchange(way):
        turn = (lambda items: items[::-1]) if way else (lambda items: items)
        mirror = lambda p, n: (n - 1 - p) if way else p
        piece = lax.rem(zz, groups)
        block_decay = jnp.exp(-rt[piece] * float(tokens))
        row_decay = jnp.exp(-rt[piece] * float(tokens * nz))

        first = [
            copy(states.at[way, lax.rem(target, groups)], z_buf.at[way, zz], way, i, (at(yy, target), column))
            for i, target in enumerate(z_targets)
        ]
        for one in first:
            one.start()
        z_buf[way, zz] = states[way, piece]
        yield
        for one in first:
            one.wait_recv()
        total = jnp.zeros((MODES, LANES), F32)
        enter = {}
        for z in turn(list(range(nz))):
            enter[z] = total
            total = block_decay * total + z_buf[way, z]
        t_out[way] = total
        base = nz - 1
        second = [
            copy(t_out.at[way], y_buf.at[way, yy], way, base + i, (at(target, zz), column))
            for i, target in enumerate(y_targets)
        ]
        for one in second:
            one.start()
        yield
        for z in range(nz):
            p_buf[z] = enter[z]
        y_buf[way, yy] = total
        reached = [lax.rem(zz + nz - groups // 2 + i, nz) for i in range(groups)]
        decays_to = [jnp.exp(-rt[piece] * (mirror(z, nz) * tokens).astype(F32)) for z in reached]
        entering = [p_buf[z] for z in reached]
        for one in second:
            one.wait_recv()
        above = jnp.zeros((MODES, LANES), F32)
        for y_ in turn(list(range(ny))):
            is_before = (y_ > yy) if way else (y_ < yy)
            above = jnp.where(is_before, row_decay * above + y_buf[way, y_], above)
        base = base + ny - 1
        third = []
        for i, z in enumerate(reached):
            result = entering[i] + decays_to[i] * above
            if i == groups // 2:
                own = result
            else:
                number = len(third)
                in_out[way, number] = result
                one = copy(in_out.at[way, number], incoming.at[way, piece], way, base + number, (at(yy, z), column))
                one.start()
                third.append(one)
        incoming[way, piece] = own
        yield
        for one in third:
            one.wait_recv()
        yield

    forward = exchange(0)
    next(forward)

    @pl.loop(0, groups)
    def _(c):
        for m in range(MODES):
            w = wide(residue_v[pl.ds(m, 1), cols(c)])
            r = wide(rate_v[pl.ds(m, 1), cols(c)])
            w_t[c, m] = w
            cf_t[c, m] = w * jnp.exp(-r * (segf * float(steps) + 1.0))
            cb_t[c, m] = w * jnp.exp(-r * (float(tokens - steps + 1) - segf * float(steps)))

    @pl.loop(0, groups)
    def _(c):
        lam = [lam_t[c, m] for m in range(MODES)]
        w = [w_t[c, m] for m in range(MODES)]

        def block(jb, state):
            values = [u[c, token_rows(jb * STEP + n), :] for n in range(STEP)]
            results = []
            for value in values:
                state = [lam[m] * state[m] + value for m in range(MODES)]
                results.append(add_up([w[m] * state[m] for m in range(MODES)]))
            for n in range(STEP):
                y[c, token_rows(jb * STEP + n), :] = results[n]
            return state

        lax.fori_loop(0, steps // STEP, block, [ex_t[c, m] for m in range(MODES)])

    for load in loads[3:]:
        load.wait()
    spread(qb, qf)
    spread(cb, sf, gain_v)
    sq[...] = jnp.zeros_like(sq)
    cs[...] = jnp.zeros_like(cs)
    next(forward)
    next(forward)
    next(forward)

    @pl.loop(0, groups)
    def _(c):
        lam = [lam_t[c, m] for m in range(MODES)]
        start = [cf_t[c, m] * wide(incoming[0, c, pl.ds(m, 1), :]) for m in range(MODES)]

        def block(jb, state):
            here = [jb * STEP + n for n in range(STEP)]
            old = [y[c, token_rows(j), :] for j in here]
            qs = [qf[c, token_rows(j), :] for j in here]
            ss = [sf[c, token_rows(j), :] for j in here]
            sq_old = [sq[j] for j in here]
            cs_old = [cs[j] for j in here]
            conv = []
            for n in range(STEP):
                conv.append(old[n] + add_up(state))
                state = [lam[m] * state[m] for m in range(MODES)]
            mixed = [a * b for a, b in zip(qs, conv)]
            sq_new = [a + b * b for a, b in zip(sq_old, mixed)]
            cs_new = [a + b * d for a, b, d in zip(cs_old, mixed, ss)]
            for n, j in enumerate(here):
                y[c, token_rows(j), :] = conv[n]
                sq[j] = sq_new[n]
                cs[j] = cs_new[n]
            return state

        lax.fori_loop(0, steps // STEP, block, start)

    packed = jnp.zeros((SUB, LANES), F32)

    def pack(jb, packed):
        for inner in range(4):
            j = jb * 4 + inner
            packed = jnp.where(lane == j, jnp.sum(sq[j], axis=1, keepdims=True), packed)
            packed = jnp.where(lane == j + steps, jnp.sum(cs[j], axis=1, keepdims=True), packed)
        return packed

    packed = lax.fori_loop(0, steps // 4, pack, packed)
    msg[...] = packed
    posts = [
        pltpu.make_async_remote_copy(
            src_ref=msg,
            dst_ref=tp_buf.at[i - 1],
            send_sem=tp_send.at[i - 1],
            recv_sem=tp_recv.at[i - 1],
            device_id=(place, mates[i - 1]),
            device_id_type=MESH,
        )
        for i in range(1, ntp)
    ]
    for post in posts:
        post.start()
    for post in posts:
        post.wait_recv()
    sends.extend(posts)
    sums = add_up([packed] + [tp_buf[i] for i in range(ntp - 1)]) * (1.0 / total_width)
    inv = 1.0 / jnp.sqrt(sums + 1e-06)
    proj = pltpu.roll(sums, LANES - steps, 1) * (inv * inv * inv)
    for j in range(steps):
        inv_t[j] = jnp.broadcast_to(inv[:, j : j + 1], (SUB, LANES))
        proj_t[j] = jnp.broadcast_to(proj[:, j : j + 1], (SUB, LANES))

    @pl.loop(0, groups)
    def _(c):
        lam, lam4 = decays(c)

        def block(jb, state):
            here = [steps - 1 - (jb * STEP + n) for n in range(STEP)]
            qs = [qf[c, token_rows(j), :] for j in here]
            convs = [y[c, token_rows(j), :] for j in here]
            ss = [sf[c, token_rows(j), :] for j in here]
            invs = [inv_t[j] for j in here]
            projs = [proj_t[j] for j in here]
            values = [
                (i * s - q * v * p) * q for q, v, s, i, p in zip(qs, convs, ss, invs, projs)
            ]
            state = accumulate(lam, lam4, state, values)
            for n, j in enumerate(here):
                cg[c, token_rows(j), :] = values[n]
            return state

        state = lax.fori_loop(0, steps // STEP, block, [jnp.zeros((SUB, LANES), F32)] * MODES)
        gather_segments(c, state, True)

    backward = exchange(1)
    next(backward)

    @pl.loop(0, groups)
    def _(c):
        lam = [lam_t[c, m] for m in range(MODES)]
        w = [w_t[c, m] for m in range(MODES)]

        def block(jb, state):
            here = [steps - 1 - (jb * STEP + n) for n in range(STEP)]
            values = [cg[c, token_rows(j), :] for j in here]
            results = []
            for value in values:
                state = [lam[m] * state[m] + value for m in range(MODES)]
                results.append(add_up([w[m] * state[m] for m in range(MODES)]))
            for n, j in enumerate(here):
                u[c, token_rows(j), :] = results[n]
            return state

        lax.fori_loop(0, steps // STEP, block, [ex_t[c, m] for m in range(MODES)])

    @pl.loop(0, groups)
    def _(c):
        scale = wide(gain_v[pl.ds(c, 1), :])

        def block(jb, carry):
            here = [jb * STEP + n for n in range(STEP)]
            convs = [y[c, token_rows(j), :] for j in here]
            mixed = [qf[c, token_rows(j), :] * v for j, v in zip(here, convs)]
            invs = [inv_t[j] for j in here]
            grads = [
                (i * sf[c, token_rows(j), :] - x * proj_t[j]) * v for j, i, x, v in zip(here, invs, mixed, convs)
            ]
            for n, j in enumerate(here):
                nm[c, token_rows(j), :] = mixed[n] * invs[n] * scale
                qg[c, token_rows(j), :] = grads[n]
            return carry

        lax.fori_loop(0, steps // STEP, block, 0)

    def round_out(src, dst):
        @pl.loop(0, groups)
        def _(c):
            for n in range(SUB):
                dst[n * steps : (n + 1) * steps, cols(c)] = src[c, pl.ds(n * (steps + PAD), steps), :].astype(dst.dtype)

    round_out(nm, normed)
    round_out(qg, query_grad)
    next(backward)
    next(backward)
    next(backward)
    behind[...] = incoming[1]
    for one in sends:
        one.wait_send()


def finish(normed_v, query_v, u, behind, lam_t, cb_t, normed, query_grad, gated_grad, out, full, sem):
    groups = u.shape[0]
    tokens = out.shape[0]
    steps = tokens // SUB
    early = [
        pltpu.make_async_copy(normed_v, normed, sem.at[0]),
        pltpu.make_async_copy(query_v, query_grad, sem.at[1]),
    ]
    for one in early:
        one.start()
    late = []
    share = groups // PARTS
    for number in range(PARTS):

        @pl.loop(number * share, (number + 1) * share)
        def _(c):
            lam = [lam_t[c, m] for m in range(MODES)]
            start = [
                cb_t[c, m] * jnp.broadcast_to(behind[c, pl.ds(m, 1), :], (SUB, LANES)) for m in range(MODES)
            ]

            def block(jb, state):
                here = [pl.ds(steps - 1 - (jb * STEP + n), SUB, stride=steps + PAD) for n in range(STEP)]
                results = []
                for old in [u[c, rows, :] for rows in here]:
                    results.append(old + add_up(state))
                    state = [lam[m] * state[m] for m in range(MODES)]
                for n, rows in enumerate(here):
                    full[c, rows, :] = results[n]
                return state

            lax.fori_loop(0, steps // STEP, block, start)
            cols = pl.ds(pl.multiple_of(c * LANES, LANES), LANES)
            for n in range(SUB):
                out[n * steps : (n + 1) * steps, cols] = full[c, pl.ds(n * (steps + PAD), steps), :].astype(out.dtype)

        span = pl.ds(number * share * LANES, share * LANES)
        one = pltpu.make_async_copy(out.at[:, span], gated_grad.at[:, span], sem.at[2 + number])
        one.start()
        late.append(one)
    for one in early + late:
        one.wait()


def shape_of(ctx):
    return ctx // 16, 16


def solution(mesh):
    ntp, ctx = mesh.shape["tp"], mesh.shape["ctx"]
    ny, nz = shape_of(ctx)

    def per_device(query, gated, cotangent, rate, residue, gain):
        tokens, width = query.shape
        groups = width // LANES
        steps = tokens // SUB
        vmem = lambda *shape: pltpu.VMEM(shape, F32)
        half = pltpu.VMEM((tokens, width), jnp.bfloat16)
        copies = (nz - 1) + (ny - 1) + (groups - 1)
        anywhere = pl.BlockSpec(memory_space=pl.ANY)
        in_vmem = pl.BlockSpec(memory_space=pltpu.VMEM)
        states = vmem(groups, MODES, SUB, LANES)
        values = vmem(groups, tokens + SUB * PAD, LANES)
        held = pl.pallas_call(
            functools.partial(kernel, ny, nz, ntp),
            out_shape=[half, half, values, vmem(groups, MODES, LANES), states, states],
            in_specs=[anywhere] * 6,
            out_specs=[in_vmem] * 6,
            scratch_shapes=[half] * 3
            + [vmem(MODES, width), vmem(MODES, width), vmem(groups, LANES)]
            + [values] * 6
            + [vmem(groups, MODES, LANES)]
            + [states] * 3
            + [
                vmem(2, groups, MODES, LANES),
                vmem(2, groups, MODES, LANES),
                vmem(2, nz, MODES, LANES),
                vmem(2, ny, MODES, LANES),
                vmem(2, MODES, LANES),
                vmem(2, groups - 1, MODES, LANES),
                vmem(nz, MODES, LANES),
            ]
            + [vmem(steps, SUB, LANES)] * 2
            + [vmem(SUB, LANES), vmem(max(ntp - 1, 1), SUB, LANES)]
            + [vmem(steps, SUB, LANES)] * 2
            + [
                pltpu.SemaphoreType.DMA((6,)),
                pltpu.SemaphoreType.DMA((2, copies)),
                pltpu.SemaphoreType.DMA((2, copies)),
                pltpu.SemaphoreType.DMA((max(ntp - 1, 1),)),
                pltpu.SemaphoreType.DMA((max(ntp - 1, 1),)),
            ],
            compiler_params=pltpu.CompilerParams(collective_id=0, has_side_effects=True),
            name="hyena",
        )(query, gated, cotangent, rate.T, residue.T, gain.reshape(groups, LANES))
        return pl.pallas_call(
            finish,
            out_shape=[jax.ShapeDtypeStruct((tokens, width), jnp.bfloat16)] * 3,
            in_specs=[in_vmem] * 6,
            out_specs=[anywhere] * 3,
            scratch_shapes=[half, values, pltpu.SemaphoreType.DMA((2 + PARTS,))],
            name="finish",
        )(*[pltpu.with_memory_space_constraint(one, pltpu.VMEM) for one in held])

    return jax.shard_map(
        per_device,
        mesh=mesh,
        in_specs=(P("ctx", "tp"), P("ctx", "tp"), P("ctx", "tp"), P("tp", None), P("tp", None), P("tp")),
        out_specs=(P("ctx", "tp"),) * 3,
        check_vma=False,
    )
```

```python
import functools

import jax
import jax.numpy as jnp
from jax import lax
from jax.experimental import pallas as pl
from jax.experimental.pallas import tpu as pltpu
from jax.sharding import PartitionSpec as P

MESH = pl.DeviceIdType.MESH
MODES = 8
SUB = 8
LANES = 128
PAD = 4
ORDER = (0, 1, 7, 2, 6, 3, 5, 4)
NEAREST = (0, 1, -1, 2, -2, 3, -3, -4)
STEP = 8
F32 = jnp.float32


def add_up(terms):
    while len(terms) > 1:
        terms = [a + b for a, b in zip(terms[::2], terms[1::2])] + ([terms[-1]] if len(terms) % 2 else [])
    return terms[0]


def kernel(
    ny, nz, ntp,
    query, gated, cotangent, rate, residue, gain,
    normed, query_grad, gated_grad,
    qb, gb, cb, rate_v, residue_v, gain_v,
    u, y, qf, sf, cg, nm, qg,
    rt, lam_t, w_t, cf_t, cb_t, ex_t,
    states, incoming, z_buf, y_buf, t_out, in_out, p_buf,
    sq, cs, msg, tp_buf, inv_t, proj_t,
    in_sem, send_sem, recv_sem, tp_send, tp_recv,
):
    tokens, width = qb.shape
    groups = width // LANES
    steps = tokens // SUB
    seq_total = tokens * nz * ny
    total_width = width * ntp
    place = lax.axis_index("ctx")
    column = lax.axis_index("tp")
    yy = place // nz
    zz = lax.rem(place, nz)

    def at(y_, z_):
        return y_ * nz + z_

    z_targets = [lax.rem(zz + i, nz) for i in range(1, nz)]
    y_targets = [lax.rem(yy + i, ny) for i in range(1, ny)]
    mates = [lax.rem(column + i, ntp) for i in range(1, ntp)]

    barrier = pltpu.get_barrier_semaphore()
    for other in [at(yy, z) for z in z_targets] + [at(y_, zz) for y_ in y_targets]:
        pl.semaphore_signal(barrier, inc=1, device_id=(other, column), device_id_type=MESH)
    for mate in mates:
        pl.semaphore_signal(barrier, inc=1, device_id=(place, mate), device_id_type=MESH)

    loads = [
        pltpu.make_async_copy(src, dst, in_sem.at[n])
        for n, (src, dst) in enumerate(
            [(rate, rate_v), (residue, residue_v), (gated, gb), (query, qb), (cotangent, cb), (gain, gain_v)]
        )
    ]
    for load in loads:
        load.start()

    seg = lax.broadcasted_iota(jnp.int32, (SUB, LANES), 0)
    segf = seg.astype(F32)
    lane = lax.broadcasted_iota(jnp.int32, (SUB, LANES), 1)

    def cols(c):
        return pl.ds(pl.multiple_of(c * LANES, LANES), LANES)

    def wide(row):
        return jnp.broadcast_to(row, (SUB, LANES))

    def token_rows(j):
        return pl.ds(j, SUB, stride=steps + PAD)

    def spread(src, dst, scale=None):
        @pl.loop(0, groups)
        def _(c):
            for n in range(SUB):
                tile = src[n * steps : (n + 1) * steps, cols(c)].astype(F32)
                dst[c, pl.ds(n * (steps + PAD), steps), :] = tile if scale is None else tile * scale[pl.ds(c, 1), :]

    def gather_segments(c, state, reverse):
        for m in range(MODES):
            r = wide(rate_v[pl.ds(m, 1), cols(c)])
            x = state[m]
            for hop in (1, 2, 4):
                decay = jnp.exp(-r * float(steps * hop))
                if reverse:
                    x = x + jnp.where(seg < SUB - hop, decay, 0.0) * pltpu.roll(x, SUB - hop, 0)
                else:
                    x = x + jnp.where(seg >= hop, decay, 0.0) * pltpu.roll(x, hop, 0)
            if reverse:
                states[1, c, pl.ds(m, 1), :] = x[0:1]
                ex_t[c, m] = jnp.where(seg < SUB - 1, pltpu.roll(x, SUB - 1, 0), 0.0)
            else:
                states[0, c, pl.ds(m, 1), :] = x[SUB - 1 : SUB]
                ex_t[c, m] = jnp.where(seg >= 1, pltpu.roll(x, 1, 0), 0.0)

    def decays(c):
        lam = [lam_t[c, m] for m in range(MODES)]
        lam4 = [a * a for a in lam]
        return lam, [a * a for a in lam4]

    def accumulate(lam, lam4, state, values):
        for n in range(0, len(values), 4):
            fresh = [
                (lam[m] * values[n] + values[n + 1]) * (lam[m] * lam[m]) + (lam[m] * values[n + 2] + values[n + 3])
                for m in range(MODES)
            ]
            state = [lam4[m] * state[m] + fresh[m] for m in range(MODES)]
        return state

    loads[0].wait()
    loads[1].wait()

    @pl.loop(0, groups)
    def _(c):
        rates = rate_v[:, cols(c)]
        rt[c] = rates
        residue_v[:, cols(c)] = residue_v[:, cols(c)] * jnp.sqrt(2.0 * rates + 1.0 / seq_total)
        for m in range(MODES):
            lam_t[c, m] = jnp.exp(-wide(rate_v[pl.ds(m, 1), cols(c)]))

    loads[2].wait()
    spread(gb, u)

    sends = []

    def copy(src, dst, way, number, device):
        out = pltpu.make_async_remote_copy(
            src_ref=src,
            dst_ref=dst,
            send_sem=send_sem.at[way, number],
            recv_sem=recv_sem.at[way, number],
            device_id=device,
            device_id_type=MESH,
        )
        sends.append(out)
        return out

    def exchange(way):
        turn = (lambda items: items[::-1]) if way else (lambda items: items)
        mirror = lambda p, n: (n - 1 - p) if way else p
        piece = lax.rem(zz, groups)
        first = []
        block_decay = jnp.exp(-rt[piece] * float(tokens))
        row_decay = jnp.exp(-rt[piece] * float(tokens * nz))

        for shift in ORDER:
            c = lax.rem(zz + shift, groups)
            for i in (shift, shift + groups):
                if i == 0:
                    continue
                one = copy(states.at[way, c], z_buf.at[way, zz], way, i - 1, (at(yy, z_targets[i - 1]), column))
                one.start()
                first.append(one)
            yield
        z_buf[way, zz] = states[way, piece]
        for one in first:
            one.wait_recv()
        total = jnp.zeros((MODES, LANES), F32)
        enter = {}
        for z in turn(list(range(nz))):
            enter[z] = total
            total = block_decay * total + z_buf[way, z]
        t_out[way] = total
        base = nz - 1
        second = [
            copy(t_out.at[way], y_buf.at[way, yy], way, base + i, (at(target, zz), column))
            for i, target in enumerate(y_targets)
        ]
        for one in second:
            one.start()
        yield
        for z in range(nz):
            p_buf[z] = enter[z]
        y_buf[way, yy] = total
        reached = [lax.rem(zz + nz + e, nz) for e in NEAREST]
        decays_to = [jnp.exp(-rt[piece] * (mirror(z, nz) * tokens).astype(F32)) for z in reached]
        entering = [p_buf[z] for z in reached]
        for one in second:
            one.wait_recv()
        above = jnp.zeros((MODES, LANES), F32)
        for y_ in turn(list(range(ny))):
            is_before = (y_ > yy) if way else (y_ < yy)
            above = jnp.where(is_before, row_decay * above + y_buf[way, y_], above)
        base = base + ny - 1
        third = [None] * groups
        for i in reversed(range(groups)):
            result = entering[i] + decays_to[i] * above
            if i == 0:
                incoming[way, piece] = result
            else:
                in_out[way, i - 1] = result
                third[i] = copy(
                    in_out.at[way, i - 1], incoming.at[way, piece], way, base + i - 1, (at(yy, reached[i]), column)
                )
                third[i].start()
        for i in range(groups):
            yield
            if i:
                third[i].wait_recv()
        yield

    def arriving(i):
        return lax.rem(zz + 2 * groups - NEAREST[i], groups)

    def forward_states(c):
        lam, lam4 = decays(c)

        def block(jb, state):
            values = [u[c, token_rows(jb * STEP + n), :] for n in range(STEP)]
            return accumulate(lam, lam4, state, values)

        state = lax.fori_loop(0, steps // STEP, block, [jnp.zeros((SUB, LANES), F32)] * MODES)
        gather_segments(c, state, False)

    forward = exchange(0)
    early = groups // 2
    for shift in ORDER[:early]:
        forward_states(lax.rem(zz + shift, groups))
    pl.semaphore_wait(barrier, len(z_targets) + len(y_targets) + len(mates))
    for _ in range(early):
        next(forward)
    for shift in ORDER[early:]:
        forward_states(lax.rem(zz + shift, groups))
        next(forward)

    @pl.loop(0, groups)
    def _(c):
        for m in range(MODES):
            w = wide(residue_v[pl.ds(m, 1), cols(c)])
            r = wide(rate_v[pl.ds(m, 1), cols(c)])
            w_t[c, m] = w
            cf_t[c, m] = w * jnp.exp(-r * (segf * float(steps) + 1.0))
            cb_t[c, m] = w * jnp.exp(-r * (float(tokens - steps + 1) - segf * float(steps)))

    for load in loads[3:]:
        load.wait()
    spread(qb, qf)
    spread(cb, sf, gain_v)
    sq[...] = jnp.zeros_like(sq)
    cs[...] = jnp.zeros_like(cs)
    next(forward)

    @pl.loop(0, groups)
    def _(c):
        lam = [lam_t[c, m] for m in range(MODES)]
        w = [w_t[c, m] for m in range(MODES)]

        def block(jb, state):
            values = [u[c, token_rows(jb * STEP + n), :] for n in range(STEP)]
            results = []
            for value in values:
                state = [lam[m] * state[m] + value for m in range(MODES)]
                results.append(add_up([w[m] * state[m] for m in range(MODES)]))
            for n in range(STEP):
                y[c, token_rows(jb * STEP + n), :] = results[n]
            return state

        lax.fori_loop(0, steps // STEP, block, [ex_t[c, m] for m in range(MODES)])

    next(forward)

    def add_earlier(c):
        lam = [lam_t[c, m] for m in range(MODES)]
        start = [cf_t[c, m] * wide(incoming[0, c, pl.ds(m, 1), :]) for m in range(MODES)]

        def block(jb, state):
            here = [jb * STEP + n for n in range(STEP)]
            old = [y[c, token_rows(j), :] for j in here]
            qs = [qf[c, token_rows(j), :] for j in here]
            ss = [sf[c, token_rows(j), :] for j in here]
            sq_old = [sq[j] for j in here]
            cs_old = [cs[j] for j in here]
            conv = []
            for n in range(STEP):
                conv.append(old[n] + add_up(state))
                state = [lam[m] * state[m] for m in range(MODES)]
            mixed = [a * b for a, b in zip(qs, conv)]
            sq_new = [a + b * b for a, b in zip(sq_old, mixed)]
            cs_new = [a + b * d for a, b, d in zip(cs_old, mixed, ss)]
            for n, j in enumerate(here):
                y[c, token_rows(j), :] = conv[n]
                sq[j] = sq_new[n]
                cs[j] = cs_new[n]
            return state

        lax.fori_loop(0, steps // STEP, block, start)

    for i in range(groups):
        next(forward)
        add_earlier(arriving(i))

    packed = jnp.zeros((SUB, LANES), F32)

    def pack(jb, packed):
        for inner in range(4):
            j = jb * 4 + inner
            packed = jnp.where(lane == j, jnp.sum(sq[j], axis=1, keepdims=True), packed)
            packed = jnp.where(lane == j + steps, jnp.sum(cs[j], axis=1, keepdims=True), packed)
        return packed

    packed = lax.fori_loop(0, steps // 4, pack, packed)
    msg[...] = packed
    posts = [
        pltpu.make_async_remote_copy(
            src_ref=msg,
            dst_ref=tp_buf.at[i - 1],
            send_sem=tp_send.at[i - 1],
            recv_sem=tp_recv.at[i - 1],
            device_id=(place, mates[i - 1]),
            device_id_type=MESH,
        )
        for i in range(1, ntp)
    ]
    for post in posts:
        post.start()
    for post in posts:
        post.wait_recv()
    sends.extend(posts)
    sums = add_up([packed] + [tp_buf[i] for i in range(ntp - 1)]) * (1.0 / total_width)
    inv = 1.0 / jnp.sqrt(sums + 1e-06)
    proj = pltpu.roll(sums, LANES - steps, 1) * (inv * inv * inv)
    for j in range(steps):
        inv_t[j] = jnp.broadcast_to(inv[:, j : j + 1], (SUB, LANES))
        proj_t[j] = jnp.broadcast_to(proj[:, j : j + 1], (SUB, LANES))

    def gradient_states(c):
        lam, lam4 = decays(c)

        def block(jb, state):
            here = [steps - 1 - (jb * STEP + n) for n in range(STEP)]
            qs = [qf[c, token_rows(j), :] for j in here]
            convs = [y[c, token_rows(j), :] for j in here]
            ss = [sf[c, token_rows(j), :] for j in here]
            invs = [inv_t[j] for j in here]
            projs = [proj_t[j] for j in here]
            values = [
                (i * s - q * v * p) * q for q, v, s, i, p in zip(qs, convs, ss, invs, projs)
            ]
            state = accumulate(lam, lam4, state, values)
            for n, j in enumerate(here):
                cg[c, token_rows(j), :] = values[n]
            return state

        state = lax.fori_loop(0, steps // STEP, block, [jnp.zeros((SUB, LANES), F32)] * MODES)
        gather_segments(c, state, True)

    backward = exchange(1)
    for shift in ORDER:
        gradient_states(lax.rem(zz + shift, groups))
        next(backward)

    @pl.loop(0, groups)
    def _(c):
        lam = [lam_t[c, m] for m in range(MODES)]
        w = [w_t[c, m] for m in range(MODES)]

        def block(jb, state):
            here = [steps - 1 - (jb * STEP + n) for n in range(STEP)]
            values = [cg[c, token_rows(j), :] for j in here]
            results = []
            for value in values:
                state = [lam[m] * state[m] + value for m in range(MODES)]
                results.append(add_up([w[m] * state[m] for m in range(MODES)]))
            for n, j in enumerate(here):
                u[c, token_rows(j), :] = results[n]
            return state

        lax.fori_loop(0, steps // STEP, block, [ex_t[c, m] for m in range(MODES)])

    @pl.loop(0, groups)
    def _(c):
        scale = wide(gain_v[pl.ds(c, 1), :])

        def block(jb, carry):
            here = [jb * STEP + n for n in range(STEP)]
            convs = [y[c, token_rows(j), :] for j in here]
            mixed = [qf[c, token_rows(j), :] * v for j, v in zip(here, convs)]
            invs = [inv_t[j] for j in here]
            grads = [
                (i * sf[c, token_rows(j), :] - x * proj_t[j]) * v for j, i, x, v in zip(here, invs, mixed, convs)
            ]
            for n, j in enumerate(here):
                nm[c, token_rows(j), :] = mixed[n] * invs[n] * scale
                qg[c, token_rows(j), :] = grads[n]
            return carry

        lax.fori_loop(0, steps // STEP, block, 0)

    def round_out(src, dst):
        @pl.loop(0, groups)
        def _(c):
            for n in range(SUB):
                dst[n * steps : (n + 1) * steps, cols(c)] = src[c, pl.ds(n * (steps + PAD), steps), :].astype(dst.dtype)

    round_out(nm, normed)
    round_out(qg, query_grad)
    next(backward)
    next(backward)

    def add_later(c):
        lam = [lam_t[c, m] for m in range(MODES)]
        start = [cb_t[c, m] * wide(incoming[1, c, pl.ds(m, 1), :]) for m in range(MODES)]

        def block(jb, state):
            here = [steps - 1 - (jb * STEP + n) for n in range(STEP)]
            results = []
            for old in [u[c, token_rows(j), :] for j in here]:
                results.append(old + add_up(state))
                state = [lam[m] * state[m] for m in range(MODES)]
            for n, j in enumerate(here):
                u[c, token_rows(j), :] = results[n]
            return state

        lax.fori_loop(0, steps // STEP, block, start)
        for n in range(SUB):
            gated_grad[n * steps : (n + 1) * steps, cols(c)] = u[c, pl.ds(n * (steps + PAD), steps), :].astype(
                gated_grad.dtype
            )

    for i in range(groups):
        next(backward)
        add_later(arriving(i))
    for one in sends:
        one.wait_send()


def finish(normed_v, query_v, gated_v, normed, query_grad, gated_grad, sem):
    pairs = [(normed_v, normed), (query_v, query_grad), (gated_v, gated_grad)]
    stores = [pltpu.make_async_copy(src, dst, sem.at[n]) for n, (src, dst) in enumerate(pairs)]
    for store in stores:
        store.start()
    for store in stores:
        store.wait()


def shape_of(ctx):
    return ctx // 16, 16


def solution(mesh):
    ntp, ctx = mesh.shape["tp"], mesh.shape["ctx"]
    ny, nz = shape_of(ctx)

    def per_device(query, gated, cotangent, rate, residue, gain):
        tokens, width = query.shape
        groups = width // LANES
        steps = tokens // SUB
        vmem = lambda *shape: pltpu.VMEM(shape, F32)
        half = pltpu.VMEM((tokens, width), jnp.bfloat16)
        copies = (nz - 1) + (ny - 1) + (groups - 1)
        anywhere = pl.BlockSpec(memory_space=pl.ANY)
        in_vmem = pl.BlockSpec(memory_space=pltpu.VMEM)
        states = vmem(groups, MODES, SUB, LANES)
        values = vmem(groups, tokens + SUB * PAD, LANES)
        held = pl.pallas_call(
            functools.partial(kernel, ny, nz, ntp),
            out_shape=[half] * 3,
            in_specs=[anywhere] * 6,
            out_specs=[in_vmem] * 3,
            scratch_shapes=[half] * 3
            + [vmem(MODES, width), vmem(MODES, width), vmem(groups, LANES)]
            + [values] * 7
            + [vmem(groups, MODES, LANES)]
            + [states] * 5
            + [
                vmem(2, groups, MODES, LANES),
                vmem(2, groups, MODES, LANES),
                vmem(2, nz, MODES, LANES),
                vmem(2, ny, MODES, LANES),
                vmem(2, MODES, LANES),
                vmem(2, groups - 1, MODES, LANES),
                vmem(nz, MODES, LANES),
            ]
            + [vmem(steps, SUB, LANES)] * 2
            + [vmem(SUB, LANES), vmem(max(ntp - 1, 1), SUB, LANES)]
            + [vmem(steps, SUB, LANES)] * 2
            + [
                pltpu.SemaphoreType.DMA((6,)),
                pltpu.SemaphoreType.DMA((2, copies)),
                pltpu.SemaphoreType.DMA((2, copies)),
                pltpu.SemaphoreType.DMA((max(ntp - 1, 1),)),
                pltpu.SemaphoreType.DMA((max(ntp - 1, 1),)),
            ],
            compiler_params=pltpu.CompilerParams(collective_id=0, has_side_effects=True),
            name="hyena",
        )(query, gated, cotangent, rate.T, residue.T, gain.reshape(groups, LANES))
        return pl.pallas_call(
            finish,
            out_shape=[jax.ShapeDtypeStruct((tokens, width), jnp.bfloat16)] * 3,
            in_specs=[in_vmem] * 3,
            out_specs=[anywhere] * 3,
            scratch_shapes=[pltpu.SemaphoreType.DMA((3,))],
            name="finish",
        )(*[pltpu.with_memory_space_constraint(one, pltpu.VMEM) for one in held])

    return jax.shard_map(
        per_device,
        mesh=mesh,
        in_specs=(P("ctx", "tp"), P("ctx", "tp"), P("ctx", "tp"), P("tp", None), P("tp", None), P("tp")),
        out_specs=(P("ctx", "tp"),) * 3,
        check_vma=False,
    )
```

```python
import functools

import jax
import jax.numpy as jnp
from jax import lax
from jax.experimental import pallas as pl
from jax.experimental.pallas import tpu as pltpu
from jax.sharding import PartitionSpec as P

MESH = pl.DeviceIdType.MESH
MODES = 8
SUB = 8
LANES = 128
PAD = 4
ORDER = (0, 1, 7, 2, 6, 3, 5, 4)
NEAREST = (0, 1, -1, 2, -2, 3, -3, -4)
STEP = 8
F32 = jnp.float32


def add_up(terms):
    while len(terms) > 1:
        terms = [a + b for a, b in zip(terms[::2], terms[1::2])] + ([terms[-1]] if len(terms) % 2 else [])
    return terms[0]


def kernel(
    ny, nz, ntp,
    query, gated, cotangent, rate, residue, gain,
    normed, query_grad, gated_grad,
    qb, gb, cb, rate_v, residue_v, gain_v,
    u, y, qf, sf, cg, nm, qg,
    rt, lam_t, w_t, cf_t, cb_t, ex_t,
    states, incoming, z_buf, y_buf, t_out, in_out, p_buf,
    sq, cs, msg, tp_buf, inv_t, proj_t,
    in_sem, send_sem, recv_sem, tp_send, tp_recv,
):
    tokens, width = qb.shape
    groups = width // LANES
    steps = tokens // SUB
    seq_total = tokens * nz * ny
    total_width = width * ntp
    place = lax.axis_index("ctx")
    column = lax.axis_index("tp")
    yy = place // nz
    zz = lax.rem(place, nz)

    def at(y_, z_):
        return y_ * nz + z_

    z_targets = [lax.rem(zz + i, nz) for i in range(1, nz)]
    z_targets_by = [(min(i + 1, nz - i - 1), i) for i in range(nz - 1)]
    y_targets = [lax.rem(yy + i, ny) for i in range(1, ny)]
    mates = [lax.rem(column + i, ntp) for i in range(1, ntp)]

    barrier = pltpu.get_barrier_semaphore()
    far_first = sorted(z_targets_by, reverse=True)
    for other in [at(yy, z_targets[i]) for _, i in far_first] + [at(y_, zz) for y_ in y_targets]:
        pl.semaphore_signal(barrier, inc=1, device_id=(other, column), device_id_type=MESH)
    for mate in mates:
        pl.semaphore_signal(barrier, inc=1, device_id=(place, mate), device_id_type=MESH)

    loads = [
        pltpu.make_async_copy(src, dst, in_sem.at[n])
        for n, (src, dst) in enumerate(
            [(rate, rate_v), (residue, residue_v), (gated, gb), (query, qb), (cotangent, cb), (gain, gain_v)]
        )
    ]
    for load in loads:
        load.start()

    seg = lax.broadcasted_iota(jnp.int32, (SUB, LANES), 0)
    segf = seg.astype(F32)
    lane = lax.broadcasted_iota(jnp.int32, (SUB, LANES), 1)

    def cols(c):
        return pl.ds(pl.multiple_of(c * LANES, LANES), LANES)

    def wide(row):
        return jnp.broadcast_to(row, (SUB, LANES))

    def token_rows(j):
        return pl.ds(j, SUB, stride=steps + PAD)

    def spread(src, dst, scale=None):
        @pl.loop(0, groups)
        def _(c):
            for n in range(SUB):
                tile = src[n * steps : (n + 1) * steps, cols(c)].astype(F32)
                dst[c, pl.ds(n * (steps + PAD), steps), :] = tile if scale is None else tile * scale[pl.ds(c, 1), :]

    def gather_segments(c, state, reverse):
        for m in range(MODES):
            r = wide(rate_v[pl.ds(m, 1), cols(c)])
            x = state[m]
            for hop in (1, 2, 4):
                decay = jnp.exp(-r * float(steps * hop))
                if reverse:
                    x = x + jnp.where(seg < SUB - hop, decay, 0.0) * pltpu.roll(x, SUB - hop, 0)
                else:
                    x = x + jnp.where(seg >= hop, decay, 0.0) * pltpu.roll(x, hop, 0)
            if reverse:
                states[1, c, pl.ds(m, 1), :] = x[0:1]
                ex_t[c, m] = jnp.where(seg < SUB - 1, pltpu.roll(x, SUB - 1, 0), 0.0)
            else:
                states[0, c, pl.ds(m, 1), :] = x[SUB - 1 : SUB]
                ex_t[c, m] = jnp.where(seg >= 1, pltpu.roll(x, 1, 0), 0.0)

    def decays(c):
        lam = [lam_t[c, m] for m in range(MODES)]
        lam4 = [a * a for a in lam]
        return lam, [a * a for a in lam4]

    def accumulate(lam, lam4, state, values):
        for n in range(0, len(values), 4):
            fresh = [
                (lam[m] * values[n] + values[n + 1]) * (lam[m] * lam[m]) + (lam[m] * values[n + 2] + values[n + 3])
                for m in range(MODES)
            ]
            state = [lam4[m] * state[m] + fresh[m] for m in range(MODES)]
        return state

    loads[0].wait()
    loads[1].wait()

    @pl.loop(0, groups)
    def _(c):
        rates = rate_v[:, cols(c)]
        rt[c] = rates
        residue_v[:, cols(c)] = residue_v[:, cols(c)] * jnp.sqrt(2.0 * rates + 1.0 / seq_total)
        for m in range(MODES):
            lam_t[c, m] = jnp.exp(-wide(rate_v[pl.ds(m, 1), cols(c)]))

    loads[2].wait()
    spread(gb, u)

    sends = []

    def copy(src, dst, way, number, device):
        out = pltpu.make_async_remote_copy(
            src_ref=src,
            dst_ref=dst,
            send_sem=send_sem.at[way, number],
            recv_sem=recv_sem.at[way, number],
            device_id=device,
            device_id_type=MESH,
        )
        sends.append(out)
        return out

    def exchange(way):
        turn = (lambda items: items[::-1]) if way else (lambda items: items)
        mirror = lambda p, n: (n - 1 - p) if way else p
        piece = lax.rem(zz, groups)
        first = []
        block_decay = jnp.exp(-rt[piece] * float(tokens))
        row_decay = jnp.exp(-rt[piece] * float(tokens * nz))

        for shift in ORDER:
            c = lax.rem(zz + shift, groups)
            for i in (shift, shift + groups):
                if i == 0:
                    continue
                one = copy(states.at[way, c], z_buf.at[way, zz], way, i - 1, (at(yy, z_targets[i - 1]), column))
                one.start()
                first.append(one)
            yield
        z_buf[way, zz] = states[way, piece]
        for one in first:
            one.wait_recv()
        total = jnp.zeros((MODES, LANES), F32)
        enter = {}
        for z in turn(list(range(nz))):
            enter[z] = total
            total = block_decay * total + z_buf[way, z]
        t_out[way] = total
        base = nz - 1
        second = [
            copy(t_out.at[way], y_buf.at[way, yy], way, base + i, (at(target, zz), column))
            for i, target in enumerate(y_targets)
        ]
        for one in second:
            one.start()
        yield
        for z in range(nz):
            p_buf[z] = enter[z]
        y_buf[way, yy] = total
        reached = [lax.rem(zz + nz + e, nz) for e in NEAREST]
        decays_to = [jnp.exp(-rt[piece] * (mirror(z, nz) * tokens).astype(F32)) for z in reached]
        entering = [p_buf[z] for z in reached]
        for one in second:
            one.wait_recv()
        above = jnp.zeros((MODES, LANES), F32)
        for y_ in turn(list(range(ny))):
            is_before = (y_ > yy) if way else (y_ < yy)
            above = jnp.where(is_before, row_decay * above + y_buf[way, y_], above)
        base = base + ny - 1
        third = [None] * groups
        for i in reversed(range(groups)):
            result = entering[i] + decays_to[i] * above
            if i == 0:
                incoming[way, piece] = result
            else:
                in_out[way, i - 1] = result
                third[i] = copy(
                    in_out.at[way, i - 1], incoming.at[way, piece], way, base + i - 1, (at(yy, reached[i]), column)
                )
                third[i].start()
        for i in range(groups):
            yield
            if i:
                third[i].wait_recv()
        yield

    def arriving(i):
        return lax.rem(zz + 2 * groups - NEAREST[i], groups)

    def forward_states(c):
        lam, lam4 = decays(c)

        def block(jb, state):
            values = [u[c, token_rows(jb * STEP + n), :] for n in range(STEP)]
            return accumulate(lam, lam4, state, values)

        state = lax.fori_loop(0, steps // STEP, block, [jnp.zeros((SUB, LANES), F32)] * MODES)
        gather_segments(c, state, False)

    forward = exchange(0)
    early = groups // 2
    for shift in ORDER[:early]:
        forward_states(lax.rem(zz + shift, groups))
    pl.semaphore_wait(barrier, len(z_targets) + len(y_targets) + len(mates))
    for _ in range(early):
        next(forward)
    for shift in ORDER[early:]:
        forward_states(lax.rem(zz + shift, groups))
        next(forward)

    @pl.loop(0, groups)
    def _(c):
        for m in range(MODES):
            w = wide(residue_v[pl.ds(m, 1), cols(c)])
            r = wide(rate_v[pl.ds(m, 1), cols(c)])
            w_t[c, m] = w
            cf_t[c, m] = w * jnp.exp(-r * (segf * float(steps) + 1.0))
            cb_t[c, m] = w * jnp.exp(-r * (float(tokens - steps + 1) - segf * float(steps)))

    for load in loads[3:]:
        load.wait()
    spread(qb, qf)
    spread(cb, sf, gain_v)
    sq[...] = jnp.zeros_like(sq)
    cs[...] = jnp.zeros_like(cs)
    next(forward)

    @pl.loop(0, groups)
    def _(c):
        lam = [lam_t[c, m] for m in range(MODES)]
        w = [w_t[c, m] for m in range(MODES)]

        def block(jb, state):
            values = [u[c, token_rows(jb * STEP + n), :] for n in range(STEP)]
            results = []
            for value in values:
                state = [lam[m] * state[m] + value for m in range(MODES)]
                results.append(add_up([w[m] * state[m] for m in range(MODES)]))
            for n in range(STEP):
                y[c, token_rows(jb * STEP + n), :] = results[n]
            return state

        lax.fori_loop(0, steps // STEP, block, [ex_t[c, m] for m in range(MODES)])

    next(forward)

    def add_earlier(c):
        lam = [lam_t[c, m] for m in range(MODES)]
        start = [cf_t[c, m] * wide(incoming[0, c, pl.ds(m, 1), :]) for m in range(MODES)]

        def block(jb, state):
            here = [jb * STEP + n for n in range(STEP)]
            old = [y[c, token_rows(j), :] for j in here]
            qs = [qf[c, token_rows(j), :] for j in here]
            ss = [sf[c, token_rows(j), :] for j in here]
            sq_old = [sq[j] for j in here]
            cs_old = [cs[j] for j in here]
            conv = []
            for n in range(STEP):
                conv.append(old[n] + add_up(state))
                state = [lam[m] * state[m] for m in range(MODES)]
            mixed = [a * b for a, b in zip(qs, conv)]
            sq_new = [a + b * b for a, b in zip(sq_old, mixed)]
            cs_new = [a + b * d for a, b, d in zip(cs_old, mixed, ss)]
            for n, j in enumerate(here):
                y[c, token_rows(j), :] = conv[n]
                sq[j] = sq_new[n]
                cs[j] = cs_new[n]
            return state

        lax.fori_loop(0, steps // STEP, block, start)

    for i in range(groups):
        next(forward)
        add_earlier(arriving(i))

    packed = jnp.zeros((SUB, LANES), F32)

    def pack(jb, packed):
        for inner in range(4):
            j = jb * 4 + inner
            packed = jnp.where(lane == j, jnp.sum(sq[j], axis=1, keepdims=True), packed)
            packed = jnp.where(lane == j + steps, jnp.sum(cs[j], axis=1, keepdims=True), packed)
        return packed

    packed = lax.fori_loop(0, steps // 4, pack, packed)
    msg[...] = packed
    posts = [
        pltpu.make_async_remote_copy(
            src_ref=msg,
            dst_ref=tp_buf.at[i - 1],
            send_sem=tp_send.at[i - 1],
            recv_sem=tp_recv.at[i - 1],
            device_id=(place, mates[i - 1]),
            device_id_type=MESH,
        )
        for i in range(1, ntp)
    ]
    for post in posts:
        post.start()
    for post in posts:
        post.wait_recv()
    sends.extend(posts)
    sums = add_up([packed] + [tp_buf[i] for i in range(ntp - 1)]) * (1.0 / total_width)
    inv = 1.0 / jnp.sqrt(sums + 1e-06)
    proj = pltpu.roll(sums, LANES - steps, 1) * (inv * inv * inv)
    for j in range(steps):
        inv_t[j] = jnp.broadcast_to(inv[:, j : j + 1], (SUB, LANES))
        proj_t[j] = jnp.broadcast_to(proj[:, j : j + 1], (SUB, LANES))

    def gradient_states(c):
        lam, lam4 = decays(c)

        def block(jb, state):
            here = [steps - 1 - (jb * STEP + n) for n in range(STEP)]
            qs = [qf[c, token_rows(j), :] for j in here]
            convs = [y[c, token_rows(j), :] for j in here]
            ss = [sf[c, token_rows(j), :] for j in here]
            invs = [inv_t[j] for j in here]
            projs = [proj_t[j] for j in here]
            values = [
                (i * s - q * v * p) * q for q, v, s, i, p in zip(qs, convs, ss, invs, projs)
            ]
            state = accumulate(lam, lam4, state, values)
            for n, j in enumerate(here):
                cg[c, token_rows(j), :] = values[n]
            return state

        state = lax.fori_loop(0, steps // STEP, block, [jnp.zeros((SUB, LANES), F32)] * MODES)
        gather_segments(c, state, True)

    backward = exchange(1)
    for shift in ORDER:
        gradient_states(lax.rem(zz + shift, groups))
        next(backward)

    @pl.loop(0, groups)
    def _(c):
        lam = [lam_t[c, m] for m in range(MODES)]
        w = [w_t[c, m] for m in range(MODES)]

        def block(jb, state):
            here = [steps - 1 - (jb * STEP + n) for n in range(STEP)]
            values = [cg[c, token_rows(j), :] for j in here]
            results = []
            for value in values:
                state = [lam[m] * state[m] + value for m in range(MODES)]
                results.append(add_up([w[m] * state[m] for m in range(MODES)]))
            for n, j in enumerate(here):
                u[c, token_rows(j), :] = results[n]
            return state

        lax.fori_loop(0, steps // STEP, block, [ex_t[c, m] for m in range(MODES)])

    @pl.loop(0, groups)
    def _(c):
        scale = wide(gain_v[pl.ds(c, 1), :])

        def block(jb, carry):
            here = [jb * STEP + n for n in range(STEP)]
            convs = [y[c, token_rows(j), :] for j in here]
            mixed = [qf[c, token_rows(j), :] * v for j, v in zip(here, convs)]
            invs = [inv_t[j] for j in here]
            grads = [
                (i * sf[c, token_rows(j), :] - x * proj_t[j]) * v for j, i, x, v in zip(here, invs, mixed, convs)
            ]
            for n, j in enumerate(here):
                nm[c, token_rows(j), :] = mixed[n] * invs[n] * scale
                qg[c, token_rows(j), :] = grads[n]
            return carry

        lax.fori_loop(0, steps // STEP, block, 0)

    def round_out(src, dst):
        @pl.loop(0, groups)
        def _(c):
            for n in range(SUB):
                dst[n * steps : (n + 1) * steps, cols(c)] = src[c, pl.ds(n * (steps + PAD), steps), :].astype(dst.dtype)

    round_out(nm, normed)
    round_out(qg, query_grad)

    def settle():
        while sends:
            sends.pop().wait_send()

    settle()
    next(backward)
    settle()
    next(backward)

    def add_later(c):
        lam = [lam_t[c, m] for m in range(MODES)]
        start = [cb_t[c, m] * wide(incoming[1, c, pl.ds(m, 1), :]) for m in range(MODES)]

        def block(jb, state):
            here = [steps - 1 - (jb * STEP + n) for n in range(STEP)]
            results = []
            for old in [u[c, token_rows(j), :] for j in here]:
                results.append(old + add_up(state))
                state = [lam[m] * state[m] for m in range(MODES)]
            for n, j in enumerate(here):
                u[c, token_rows(j), :] = results[n]
            return state

        lax.fori_loop(0, steps // STEP, block, start)
        for n in range(SUB):
            gated_grad[n * steps : (n + 1) * steps, cols(c)] = u[c, pl.ds(n * (steps + PAD), steps), :].astype(
                gated_grad.dtype
            )

    for i in range(groups):
        next(backward)
        add_later(arriving(i))
        if i == 0:
            settle()


def finish(normed_v, query_v, gated_v, normed, query_grad, gated_grad, sem):
    pairs = [(normed_v, normed), (query_v, query_grad), (gated_v, gated_grad)]
    stores = [pltpu.make_async_copy(src, dst, sem.at[n]) for n, (src, dst) in enumerate(pairs)]
    for store in stores:
        store.start()
    for store in stores:
        store.wait()


def shape_of(ctx):
    return ctx // 16, 16


def solution(mesh):
    ntp, ctx = mesh.shape["tp"], mesh.shape["ctx"]
    ny, nz = shape_of(ctx)

    def per_device(query, gated, cotangent, rate, residue, gain):
        tokens, width = query.shape
        groups = width // LANES
        steps = tokens // SUB
        vmem = lambda *shape: pltpu.VMEM(shape, F32)
        half = pltpu.VMEM((tokens, width), jnp.bfloat16)
        copies = (nz - 1) + (ny - 1) + (groups - 1)
        anywhere = pl.BlockSpec(memory_space=pl.ANY)
        in_vmem = pl.BlockSpec(memory_space=pltpu.VMEM)
        states = vmem(groups, MODES, SUB, LANES)
        values = vmem(groups, tokens + SUB * PAD, LANES)
        held = pl.pallas_call(
            functools.partial(kernel, ny, nz, ntp),
            out_shape=[half] * 3,
            in_specs=[anywhere] * 6,
            out_specs=[in_vmem] * 3,
            scratch_shapes=[half] * 3
            + [vmem(MODES, width), vmem(MODES, width), vmem(groups, LANES)]
            + [values] * 7
            + [vmem(groups, MODES, LANES)]
            + [states] * 5
            + [
                vmem(2, groups, MODES, LANES),
                vmem(2, groups, MODES, LANES),
                vmem(2, nz, MODES, LANES),
                vmem(2, ny, MODES, LANES),
                vmem(2, MODES, LANES),
                vmem(2, groups - 1, MODES, LANES),
                vmem(nz, MODES, LANES),
            ]
            + [vmem(steps, SUB, LANES)] * 2
            + [vmem(SUB, LANES), vmem(max(ntp - 1, 1), SUB, LANES)]
            + [vmem(steps, SUB, LANES)] * 2
            + [
                pltpu.SemaphoreType.DMA((6,)),
                pltpu.SemaphoreType.DMA((2, copies)),
                pltpu.SemaphoreType.DMA((2, copies)),
                pltpu.SemaphoreType.DMA((max(ntp - 1, 1),)),
                pltpu.SemaphoreType.DMA((max(ntp - 1, 1),)),
            ],
            compiler_params=pltpu.CompilerParams(collective_id=0, has_side_effects=True),
            name="hyena",
        )(query, gated, cotangent, rate.T, residue.T, gain.reshape(groups, LANES))
        return pl.pallas_call(
            finish,
            out_shape=[jax.ShapeDtypeStruct((tokens, width), jnp.bfloat16)] * 3,
            in_specs=[in_vmem] * 3,
            out_specs=[anywhere] * 3,
            scratch_shapes=[pltpu.SemaphoreType.DMA((3,))],
            name="finish",
        )(*[pltpu.with_memory_space_constraint(one, pltpu.VMEM) for one in held])

    return jax.shard_map(
        per_device,
        mesh=mesh,
        in_specs=(P("ctx", "tp"), P("ctx", "tp"), P("ctx", "tp"), P("tp", None), P("tp", None), P("tp")),
        out_specs=(P("ctx", "tp"),) * 3,
        check_vma=False,
    )
```
